32 devices in a mesh: row: 8 (over z, core), col: 4 (over y, x).
Axes of the slice: x: 2, y: 2, z: 4, core: 2. Of those that a mesh axis runs over, the one named last changes fastest.
Arguments:
- matrix_tiles: float32 [10, 8, 128, 20, 4, 128], P(None, 'row', None, None, 'col'), may hold values from -60715.73 to 60715.73
Outputs:
- reduced: float32 [10, 8, 128, 20, 4, 128], P(None, 'row', None, None, 'col')
The draws below stay inside these ranges and needn't reach their ends.
All inputs are finite; a program needn't handle non-finite values.
Results may differ from the reference program's by a relative error of at most 0.0003.
Values sent between devices are 32-bit elements; how exact they have to be, the bound alone decides.
A program may use at most 128 MiB of HBM per device.

```python
import jax
import jax.numpy as jnp
from jax import lax

ORDER = 10240
TILE = 128
BAND = 256
PANELS = 2
ROW_BLOCKS = 10
COL_BLOCKS = 20
N_ROW = 8
N_COL = 4


def draw_matrix_tiles(key, part):
    first_key = jax.random.fold_in(key, 11)
    common_key = jax.random.fold_in(key, 37)
    common = jax.random.uniform(common_key, (ORDER,), jnp.float32, -1.7320508, 1.7320508)
    base_values = jnp.clip(jax.random.normal(first_key, (ORDER, ORDER), jnp.float32), -6.0, 6.0)
    symmetric = (base_values + base_values.T) * 0.70710678
    symmetric = symmetric + 2.0 * common[:, None] * common[None, :]
    column_norms = jnp.sqrt(jnp.sum(symmetric * symmetric, axis=0))
    offsets = jnp.arange(BAND, dtype=jnp.int32)
    for panel_index in range(PANELS):
        start_col = panel_index * BAND
        start_row = start_col + BAND
        boost_values = 2.0 * column_norms[start_col + offsets]
        symmetric = symmetric.at[start_row + offsets, start_col + offsets].add(boost_values)
        symmetric = symmetric.at[start_col + offsets, start_row + offsets].add(boost_values)
    return symmetric.reshape(ROW_BLOCKS, N_ROW, TILE, COL_BLOCKS, N_COL, TILE)


def setup_inputs(seed: int = 0) -> dict:
    keys = jax.random.split(jax.random.key(seed), 2)
    matrix_tiles = draw_matrix_tiles(jax.random.fold_in(keys[1], 71), 0)
    return dict(matrix_tiles=matrix_tiles)


def multiply(first_matrix, second_matrix):
    return jnp.dot(first_matrix, second_matrix, precision=lax.Precision.HIGHEST, preferred_element_type=first_matrix.dtype)

def transposed_left(first_matrix, second_matrix):
    return lax.dot_general(first_matrix, second_matrix, (((0,), (0,)), ((), ())), precision=lax.Precision.HIGHEST, preferred_element_type=first_matrix.dtype)

def transposed_right(first_matrix, second_matrix):
    return lax.dot_general(first_matrix, second_matrix, (((1,), (1,)), ((), ())), precision=lax.Precision.HIGHEST, preferred_element_type=first_matrix.dtype)

def lower_inverse(matrix):
    factor = jnp.linalg.cholesky(matrix)
    identity = jnp.eye(matrix.shape[0], dtype=matrix.dtype)
    return lax.linalg.triangular_solve(factor, identity, left_side=True, lower=True)

def reflector_factors(gram_matrix, top_panel):
    inverse = lower_inverse(gram_matrix)
    top_basis = transposed_right(top_panel, inverse)
    sign_values = jnp.where(jnp.diagonal(top_basis) >= 0, -1.0, 1.0).astype(top_basis.dtype)
    shifted = top_basis - jnp.diag(sign_values)
    outer_inverse = lower_inverse(transposed_left(shifted, shifted))
    kernel = transposed_left(outer_inverse, outer_inverse)
    transform = -sign_values[:, None] * multiply(shifted, kernel)
    return (inverse, sign_values, transform)

def reference(matrix_tiles):
    tile_shape = matrix_tiles.shape
    order_size = tile_shape[0] * tile_shape[1] * tile_shape[2]
    matrix = matrix_tiles.reshape(order_size, order_size)
    for panel_index in range(PANELS):
        panel_start = panel_index * BAND
        below_start = panel_start + BAND
        panel_block = matrix[below_start:, panel_start:below_start]
        gram_matrix = transposed_left(panel_block, panel_block)
        inverse, sign_values, transform = reflector_factors(gram_matrix, panel_block[:BAND])
        basis_rows = transposed_right(panel_block, inverse)
        basis_rows = basis_rows.at[:BAND].add(-jnp.diag(sign_values))
        vectors = jnp.concatenate([jnp.zeros((below_start, BAND), matrix.dtype), basis_rows], 0)
        applied = multiply(multiply(matrix, vectors), transform)
        inner_term = multiply(transform.T, transposed_left(vectors, applied))
        updates = applied - 0.5 * multiply(vectors, inner_term)
        matrix = matrix - transposed_right(jnp.concatenate([vectors, updates], 1), jnp.concatenate([updates, vectors], 1))
    return matrix.reshape(tile_shape)
```

```python
import functools

import jax
import jax.numpy as jnp
from jax import lax
from jax.experimental import pallas as pl
from jax.experimental.pallas import tpu as pltpu
from jax.sharding import PartitionSpec as P

BAND = 256
PANELS = 2
BIG = 60 * 1024 * 1024
MESH = pl.DeviceIdType.MESH

HI = lax.Precision.HIGHEST
def mm(a, b, ca, cb):
    return lax.dot_general(a, b, (((ca,), (cb,)), ((), ())), precision=HI, preferred_element_type=jnp.float32)

def base_inverse(block):
    size = block.shape[0]
    rows = lax.broadcasted_iota(jnp.int32, (size, 2 * size), 0)
    cols = lax.broadcasted_iota(jnp.int32, (size, 2 * size), 1)
    work = jnp.concatenate([block, jnp.where(rows == cols, 1.0, 0.0)[:, :size]], 1)
    for j in range(size - 1):
        row = work[j : j + 1, :]
        scaled = row * (1.0 / row[:, j : j + 1])
        factor = jnp.where(rows[:, :1] > j, work[:, j : j + 1], 0.0)
        work = work - factor * scaled
    pivots = jnp.sum(jnp.where(rows == cols, work, 0.0), axis=1, keepdims=True)
    return work[:, size:] * (1.0 / jnp.sqrt(pivots))

def factor_inverse(matrix, base):
    size = matrix.shape[0]
    if size <= base:
        return base_inverse(matrix)
    half = size // 2
    first = factor_inverse(matrix[:half, :half], base)
    lower = mm(matrix[half:, :half], first, 1, 1)
    second = factor_inverse(matrix[half:, half:] - mm(lower, lower, 1, 1), base)
    corner = -mm(second, mm(lower, first, 1, 0), 1, 0)
    top = jnp.concatenate([first, jnp.zeros_like(first)], 1)
    return jnp.concatenate([top, jnp.concatenate([corner, second], 1)], 0)

def factor_kernel(gram_ref, top_ref, inverse_ref, shifted_ref, transform_ref, sign_ref):
    size = gram_ref.shape[0]
    inverse = factor_inverse(gram_ref[...], 64)
    inverse_ref[...] = inverse
    basis = mm(top_ref[...], inverse, 1, 1)
    rows = lax.broadcasted_iota(jnp.int32, (size, size), 0)
    cols = lax.broadcasted_iota(jnp.int32, (size, size), 1)
    on_diagonal = rows == cols
    sign_square = jnp.where(on_diagonal, jnp.where(basis >= 0, -1.0, 1.0), 0.0)
    shifted = basis - sign_square
    shifted_ref[...] = shifted
    outer = factor_inverse(mm(shifted, shifted, 0, 0), 64)
    sign_column = jnp.sum(sign_square, axis=1, keepdims=True)
    transform_ref[...] = -sign_column * mm(mm(shifted, outer, 1, 1), outer, 1, 0)
    sign_ref[...] = jnp.sum(sign_square, axis=0, keepdims=True)


def factors(gram, top):
    size = gram.shape[0]
    square = jax.ShapeDtypeStruct((size, size), jnp.float32)
    return pl.pallas_call(
        factor_kernel,
        out_shape=(square, square, square, jax.ShapeDtypeStruct((1, size), jnp.float32)),
    )(gram, top)


def multiply(first, second, first_dim=1, second_dim=0, precision=HI):
    return lax.dot_general(
        first,
        second,
        (((first_dim,), (second_dim,)), ((), ())),
        precision=precision,
        preferred_element_type=jnp.float32,
    )


def greet(axis, count):
    me = lax.axis_index(axis)
    barrier = pltpu.get_barrier_semaphore()
    for step in range(1, count):
        pl.semaphore_signal(
            barrier, inc=1, device_id={axis: lax.rem(me + step, count)}, device_id_type=MESH
        )
    pl.semaphore_wait(barrier, count - 1)
    return me


def all_reduce_kernel(axis, count, x_ref, out_ref, parts, send_sem, recv_sem, send_two, recv_two):
    me = greet(axis, count)
    copies = []
    for step in range(1, count):
        peer = lax.rem(me + step, count)
        copies.append(
            pltpu.make_async_remote_copy(
                src_ref=x_ref.at[peer],
                dst_ref=parts.at[step - 1],
                send_sem=send_sem.at[step - 1],
                recv_sem=recv_sem.at[step - 1],
                device_id={axis: peer},
                device_id_type=MESH,
            )
        )
        copies[-1].start()
    total = x_ref[me]
    for step in range(1, count):
        copies[step - 1].wait_recv()
        total = total + parts[step - 1]
    out_ref[me] = total
    second = []
    for step in range(1, count):
        peer = lax.rem(me + step, count)
        second.append(
            pltpu.make_async_remote_copy(
                src_ref=out_ref.at[me],
                dst_ref=out_ref.at[me],
                send_sem=send_two.at[step - 1],
                recv_sem=recv_two.at[step - 1],
                device_id={axis: peer},
                device_id_type=MESH,
            )
        )
        second[-1].start()
    for copy in copies:
        copy.wait_send()
    for copy in second:
        copy.wait()


def all_reduce(x, axis, collective_id):
    count = lax.axis_size(axis)
    rows, cols = x.shape
    pieces = (count, rows // count, cols)
    out = pl.pallas_call(
        functools.partial(all_reduce_kernel, axis, count),
        out_shape=jax.ShapeDtypeStruct(pieces, x.dtype),
        in_specs=[pl.BlockSpec(memory_space=pltpu.VMEM)],
        out_specs=pl.BlockSpec(memory_space=pltpu.VMEM),
        scratch_shapes=[pltpu.VMEM((count - 1,) + pieces[1:], x.dtype)]
        + [pltpu.SemaphoreType.DMA((count - 1,))] * 4,
        compiler_params=pltpu.CompilerParams(
            collective_id=collective_id, has_side_effects=True, vmem_limit_bytes=BIG
        ),
    )(x.reshape(pieces))
    return out.reshape(rows, cols)


def all_gather_kernel(axis, count, x_ref, out_ref, send_sem, recv_sem):
    me = greet(axis, count)
    copies = []
    for step in range(1, count):
        copies.append(
            pltpu.make_async_remote_copy(
                src_ref=x_ref,
                dst_ref=out_ref.at[me],
                send_sem=send_sem.at[step - 1],
                recv_sem=recv_sem.at[step - 1],
                device_id={axis: lax.rem(me + step, count)},
                device_id_type=MESH,
            )
        )
        copies[-1].start()
    out_ref[me] = x_ref[...]
    for copy in copies:
        copy.wait()


def all_gather(x, axis, collective_id):
    count = lax.axis_size(axis)
    return pl.pallas_call(
        functools.partial(all_gather_kernel, axis, count),
        out_shape=jax.ShapeDtypeStruct((count,) + x.shape, x.dtype),
        in_specs=[pl.BlockSpec(memory_space=pltpu.VMEM)],
        out_specs=pl.BlockSpec(memory_space=pltpu.VMEM),
        scratch_shapes=[pltpu.SemaphoreType.DMA((count - 1,))] * 2,
        compiler_params=pltpu.CompilerParams(
            collective_id=collective_id, has_side_effects=True, vmem_limit_bytes=BIG
        ),
    )(x)


def flatten_kernel(tiles, x_ref, out_ref):
    rows, size = out_ref.shape[0], x_ref.shape[1]
    for tile in range(tiles):
        out_ref[:, tile * size : (tile + 1) * size] = x_ref[pl.ds(tile, rows, stride=tiles), :]


def flatten(matrix_tiles):
    block_rows, _, tile_size, block_cols, _, width = matrix_tiles.shape
    flat = matrix_tiles.reshape(block_rows * tile_size * block_cols, width)
    return pl.pallas_call(
        functools.partial(flatten_kernel, block_cols),
        grid=(block_rows,),
        in_specs=[pl.BlockSpec((tile_size * block_cols, width), lambda i: (i, 0))],
        out_specs=pl.BlockSpec((tile_size, block_cols * width), lambda i: (i, 0)),
        out_shape=jax.ShapeDtypeStruct(
            (block_rows * tile_size, block_cols * width), matrix_tiles.dtype
        ),
        compiler_params=pltpu.CompilerParams(vmem_limit_bytes=BIG),
    )(flat)


def split(value):
    high = value.astype(jnp.bfloat16)
    return high, (value - high.astype(jnp.float32)).astype(jnp.bfloat16)


def update_kernel(tiles, x_ref, left_ref, right_ref, out_ref, high_ref, low_ref):
    rows = x_ref.shape[0]
    size = x_ref.shape[1] // tiles

    @pl.when(pl.program_id(0) == 0)
    def _():
        high_ref[...], low_ref[...] = split(right_ref[...])

    left_high, left_low = split(left_ref[...])
    group = 2 if tiles % 2 == 0 else 1
    for first in range(0, tiles, group):
        part = slice(first * size, (first + group) * size)
        right_high, right_low = high_ref[part, :], low_ref[part, :]
        dot = lambda a, b: lax.dot_general(
            a, b, (((1,), (1,)), ((), ())), preferred_element_type=jnp.float32
        )
        product = dot(left_high, right_high) + (
            dot(left_high, right_low) + dot(left_low, right_high)
        )
        value = x_ref[:, part] - product
        for offset in range(group):
            out_ref[pl.ds(first + offset, rows, stride=tiles), :] = value[
                :, offset * size : (offset + 1) * size
            ]


def final_update(matrix, left, right, tile_shape):
    block_rows, _, tile_size, block_cols, _, width = tile_shape
    group = 2 if block_rows % 2 == 0 else 1
    rows = group * tile_size
    depth = left.shape[1]
    out = pl.pallas_call(
        functools.partial(update_kernel, block_cols),
        grid=(block_rows // group,),
        in_specs=[
            pl.BlockSpec((rows, block_cols * width), lambda i: (i, 0)),
            pl.BlockSpec((rows, depth), lambda i: (i, 0)),
            pl.BlockSpec(
                (block_cols * width, depth), lambda i: (0, 0), pipeline_mode=pl.Buffered(1)
            ),
        ],
        out_specs=pl.BlockSpec((rows * block_cols, width), lambda i: (i, 0)),
        out_shape=jax.ShapeDtypeStruct((block_rows * tile_size * block_cols, width), matrix.dtype),
        scratch_shapes=[pltpu.VMEM((block_cols * width, depth), jnp.bfloat16)] * 2,
        compiler_params=pltpu.CompilerParams(vmem_limit_bytes=BIG),
    )(matrix, left, right)
    return out.reshape(tile_shape)


def mirror_order(pieces, block_rows, tile_size):
    stacked = jnp.stack(pieces, 0)
    stacked = stacked.reshape(len(pieces), block_rows, tile_size, stacked.shape[-1])
    return stacked.transpose(1, 0, 2, 3).reshape(-1, stacked.shape[-1])


def on_device(matrix_tiles):
    tile_shape = matrix_tiles.shape
    block_rows, _, tile_size, block_cols = tile_shape[:4]
    row_count = block_rows * tile_size
    col_count = block_cols * tile_size
    row_devices = lax.axis_size("row")
    col_devices = lax.axis_size("col")
    row_ratio = row_devices // col_devices
    row_index = lax.axis_index("row")
    col_index = lax.axis_index("col")

    def positions(count, devices, index):
        place = jnp.arange(count, dtype=jnp.int32)
        return (place // tile_size * devices + index) * tile_size + place % tile_size

    global_rows = positions(row_count, row_devices, row_index)
    global_cols = positions(col_count, col_devices, col_index)
    band_columns = jnp.arange(BAND, dtype=jnp.int32)
    panel_tiles = BAND // tile_size
    high = lax.Precision.HIGH

    def row_tiles(source, first):
        blocks = []
        for tile in range(first, first + panel_tiles):
            local_tile = tile // row_devices
            part = source[local_tile * tile_size : (local_tile + 1) * tile_size]
            blocks.append(jnp.where(row_index == tile % row_devices, part, 0.0))
        return jnp.concatenate(blocks, 0)

    matrix = flatten(matrix_tiles)
    held = -(-PANELS * panel_tiles // col_devices)
    gathered = all_gather(matrix[:, : held * tile_size], "col", 0)
    panels_rows, panels_cols = [], []
    for panel_index in range(PANELS):
        pieces = []
        for tile in range(panel_index * panel_tiles, (panel_index + 1) * panel_tiles):
            local_tile = tile // col_devices
            pieces.append(
                gathered[
                    tile % col_devices, :, local_tile * tile_size : (local_tile + 1) * tile_size
                ]
            )
        panels_rows.append(jnp.concatenate(pieces, 1))
        panels_cols.append(lax.psum(row_tiles(matrix, panel_index * panel_tiles), "row").T)

    lefts, rights = [], []
    for panel_index in range(PANELS):
        below_start = (panel_index + 1) * BAND
        last = panel_index == PANELS - 1
        panel_rows = jnp.where((global_rows >= below_start)[:, None], panels_rows[panel_index], 0.0)
        stacked = jnp.concatenate(
            [
                multiply(panel_rows, panel_rows, 0, 0),
                row_tiles(panel_rows, below_start // tile_size),
            ],
            0,
        )
        stacked = all_reduce(stacked, "row", 1)
        inverse, shifted, transform, signs = factors(stacked[:BAND], stacked[BAND:])

        def reflectors(panel, places):
            on_sign = (places[:, None] - below_start == band_columns[None, :]).astype(jnp.float32)
            return multiply(panel, inverse, 1, 1) - on_sign * signs

        vec_rows = reflectors(panel_rows, global_rows)
        panel_cols = jnp.where((global_cols >= below_start)[:, None], panels_cols[panel_index], 0.0)
        vec_cols = reflectors(panel_cols, global_cols)
        partial = multiply(matrix, vec_cols, precision=high)
        if lefts:
            left, right = jnp.concatenate(lefts, 1), jnp.concatenate(rights, 1)
            partial = partial - multiply(
                left, multiply(right, vec_cols, 0, 0, precision=high), precision=high
            )
        applied = multiply(all_reduce(partial, "col", 2), transform)
        pieces = []
        for part_index in range(row_ratio):
            mine = row_index == col_index + col_devices * part_index
            pieces.append(lax.psum(jnp.where(mine, applied, 0.0), "row"))
        applied_cols = mirror_order(pieces, block_rows, tile_size)
        inner_part = multiply(vec_rows, applied, 0, 0)
        if last:
            inner = all_reduce(inner_part, "row", 3)
        else:
            stacked = jnp.concatenate([inner_part, row_tiles(applied, below_start // tile_size)], 0)
            stacked = all_reduce(stacked, "row", 1)
            inner = stacked[:BAND]
        half_inner = 0.5 * multiply(transform, inner, 0, 0)
        update_rows = applied - multiply(vec_rows, half_inner)
        update_cols = applied_cols - multiply(vec_cols, half_inner)
        lefts += [vec_rows, update_rows]
        rights += [update_cols, vec_cols]
        if not last:
            update_next = stacked[BAND:] - multiply(shifted, half_inner)
            panels_rows[panel_index + 1] = (
                panels_rows[panel_index + 1]
                - multiply(vec_rows, update_next, 1, 1)
                - multiply(update_rows, shifted, 1, 1)
            )
            panels_cols[panel_index + 1] = (
                panels_cols[panel_index + 1]
                - multiply(vec_cols, update_next, 1, 1)
                - multiply(update_cols, shifted, 1, 1)
            )
    return final_update(
        matrix, jnp.concatenate(lefts, 1), jnp.concatenate(rights, 1), tile_shape
    )


def solution(mesh):
    return jax.shard_map(
        on_device,
        mesh=mesh,
        in_specs=(P(None, "row", None, None, "col", None),),
        out_specs=P(None, "row", None, None, "col", None),
        check_vma=False,
    )
```

```python
import functools

import jax
import jax.numpy as jnp
from jax import lax
from jax.experimental import pallas as pl
from jax.experimental.pallas import tpu as pltpu
from jax.sharding import PartitionSpec as P

BAND = 256
PANELS = 2
BIG = 60 * 1024 * 1024
MESH = pl.DeviceIdType.MESH

HI = lax.Precision.HIGHEST
def mm(a, b, ca, cb):
    return lax.dot_general(a, b, (((ca,), (cb,)), ((), ())), precision=HI, preferred_element_type=jnp.float32)

def base_inverse(block):
    size = block.shape[0]
    rows = lax.broadcasted_iota(jnp.int32, (size, 2 * size), 0)
    cols = lax.broadcasted_iota(jnp.int32, (size, 2 * size), 1)
    work = jnp.concatenate([block, jnp.where(rows == cols, 1.0, 0.0)[:, :size]], 1)
    for j in range(size - 1):
        row = work[j : j + 1, :]
        scaled = row * (1.0 / row[:, j : j + 1])
        factor = jnp.where(rows[:, :1] > j, work[:, j : j + 1], 0.0)
        work = work - factor * scaled
    pivots = jnp.sum(jnp.where(rows == cols, work, 0.0), axis=1, keepdims=True)
    return work[:, size:] * (1.0 / jnp.sqrt(pivots))

def factor_inverse(matrix, base):
    size = matrix.shape[0]
    if size <= base:
        return base_inverse(matrix)
    half = size // 2
    first = factor_inverse(matrix[:half, :half], base)
    lower = mm(matrix[half:, :half], first, 1, 1)
    second = factor_inverse(matrix[half:, half:] - mm(lower, lower, 1, 1), base)
    corner = -mm(second, mm(lower, first, 1, 0), 1, 0)
    top = jnp.concatenate([first, jnp.zeros_like(first)], 1)
    return jnp.concatenate([top, jnp.concatenate([corner, second], 1)], 0)

def factor_kernel(gram_ref, top_ref, inverse_ref, shifted_ref, transform_ref, sign_ref):
    size = gram_ref.shape[0]
    inverse = factor_inverse(gram_ref[...], 64)
    inverse_ref[...] = inverse
    basis = mm(top_ref[...], inverse, 1, 1)
    rows = lax.broadcasted_iota(jnp.int32, (size, size), 0)
    cols = lax.broadcasted_iota(jnp.int32, (size, size), 1)
    on_diagonal = rows == cols
    sign_square = jnp.where(on_diagonal, jnp.where(basis >= 0, -1.0, 1.0), 0.0)
    shifted = basis - sign_square
    shifted_ref[...] = shifted
    outer = factor_inverse(mm(shifted, shifted, 0, 0), 64)
    sign_column = jnp.sum(sign_square, axis=1, keepdims=True)
    transform_ref[...] = -sign_column * mm(mm(shifted, outer, 1, 1), outer, 1, 0)
    sign_ref[...] = jnp.sum(sign_square, axis=0, keepdims=True)


def factors(gram, top):
    size = gram.shape[0]
    square = jax.ShapeDtypeStruct((size, size), jnp.float32)
    return pl.pallas_call(
        factor_kernel,
        out_shape=(square, square, square, jax.ShapeDtypeStruct((1, size), jnp.float32)),
    )(gram, top)


def multiply(first, second, first_dim=1, second_dim=0, precision=HI):
    return lax.dot_general(
        first,
        second,
        (((first_dim,), (second_dim,)), ((), ())),
        precision=precision,
        preferred_element_type=jnp.float32,
    )


def greet(axis, count):
    me = lax.axis_index(axis)
    barrier = pltpu.get_barrier_semaphore()
    for step in range(1, count):
        pl.semaphore_signal(
            barrier, inc=1, device_id={axis: lax.rem(me + step, count)}, device_id_type=MESH
        )
    pl.semaphore_wait(barrier, count - 1)
    return me


def all_reduce_kernel(axis, count, x_ref, out_ref, parts, send_sem, recv_sem, send_two, recv_two):
    me = greet(axis, count)
    copies = []
    for step in range(1, count):
        peer = lax.rem(me + step, count)
        copies.append(
            pltpu.make_async_remote_copy(
                src_ref=x_ref.at[peer],
                dst_ref=parts.at[step - 1],
                send_sem=send_sem.at[step - 1],
                recv_sem=recv_sem.at[step - 1],
                device_id={axis: peer},
                device_id_type=MESH,
            )
        )
        copies[-1].start()
    total = x_ref[me]
    for step in range(1, count):
        copies[step - 1].wait_recv()
        total = total + parts[step - 1]
    out_ref[me] = total
    second = []
    for step in range(1, count):
        peer = lax.rem(me + step, count)
        second.append(
            pltpu.make_async_remote_copy(
                src_ref=out_ref.at[me],
                dst_ref=out_ref.at[me],
                send_sem=send_two.at[step - 1],
                recv_sem=recv_two.at[step - 1],
                device_id={axis: peer},
                device_id_type=MESH,
            )
        )
        second[-1].start()
    for copy in copies:
        copy.wait_send()
    for copy in second:
        copy.wait()


def all_reduce(x, axis, collective_id):
    count = lax.axis_size(axis)
    rows, cols = x.shape
    pieces = (count, rows // count, cols)
    out = pl.pallas_call(
        functools.partial(all_reduce_kernel, axis, count),
        out_shape=jax.ShapeDtypeStruct(pieces, x.dtype),
        in_specs=[pl.BlockSpec(memory_space=pltpu.VMEM)],
        out_specs=pl.BlockSpec(memory_space=pltpu.VMEM),
        scratch_shapes=[pltpu.VMEM((count - 1,) + pieces[1:], x.dtype)]
        + [pltpu.SemaphoreType.DMA((count - 1,))] * 4,
        compiler_params=pltpu.CompilerParams(
            collective_id=collective_id, has_side_effects=True, vmem_limit_bytes=BIG
        ),
    )(x.reshape(pieces))
    return out.reshape(rows, cols)


def share_kernel(rows, cols, x_ref, out_ref, parts, send_sem, recv_sem, send_two, recv_two, send_col, recv_col):
    row_me = lax.axis_index("row")
    col_me = lax.axis_index("col")
    barrier = pltpu.get_barrier_semaphore()
    for axis, me, count in (("row", row_me, rows), ("col", col_me, cols)):
        for step in range(1, count):
            pl.semaphore_signal(
                barrier, inc=1, device_id={axis: lax.rem(me + step, count)}, device_id_type=MESH
            )
    pl.semaphore_wait(barrier, rows + cols - 2)

    def send(source, target, axis, peer, out_sem, in_sem):
        copy = pltpu.make_async_remote_copy(
            src_ref=source,
            dst_ref=target,
            send_sem=out_sem,
            recv_sem=in_sem,
            device_id={axis: peer},
            device_id_type=MESH,
        )
        copy.start()
        return copy

    first, second, third = [], [], []
    for step in range(1, rows):
        peer = lax.rem(row_me + step, rows)
        slot = step - 1
        first.append(
            send(x_ref.at[col_me, peer], parts.at[slot], "row", peer, send_sem.at[slot], recv_sem.at[slot])
        )
    total = x_ref[col_me, row_me]
    for step in range(1, rows):
        first[step - 1].wait_recv()
        total = total + parts[step - 1]
    out_ref[col_me, row_me] = total
    mine = out_ref.at[col_me, row_me]
    for step in range(1, rows):
        peer = lax.rem(row_me + step, rows)
        slot = step - 1
        second.append(send(mine, mine, "row", peer, send_two.at[slot], recv_two.at[slot]))
    for copy in second:
        copy.wait_recv()
    mine = out_ref.at[col_me]
    for step in range(1, cols):
        peer = lax.rem(col_me + step, cols)
        slot = step - 1
        third.append(send(mine, mine, "col", peer, send_col.at[slot], recv_col.at[slot]))
    for copy in first + second:
        copy.wait_send()
    for copy in third:
        copy.wait()


def share(x, collective_id):
    rows, cols = lax.axis_size("row"), lax.axis_size("col")
    size, width = x.shape
    pieces = (cols, rows, size // (rows * cols), width)
    out = pl.pallas_call(
        functools.partial(share_kernel, rows, cols),
        out_shape=jax.ShapeDtypeStruct(pieces, x.dtype),
        in_specs=[pl.BlockSpec(memory_space=pltpu.VMEM)],
        out_specs=pl.BlockSpec(memory_space=pltpu.VMEM),
        scratch_shapes=[pltpu.VMEM((rows - 1,) + pieces[2:], x.dtype)]
        + [pltpu.SemaphoreType.DMA((rows - 1,))] * 4
        + [pltpu.SemaphoreType.DMA((cols - 1,))] * 2,
        compiler_params=pltpu.CompilerParams(
            collective_id=collective_id, has_side_effects=True, vmem_limit_bytes=BIG
        ),
    )(x.reshape(pieces))
    return out.reshape(size, width)


def all_gather_kernel(axis, count, x_ref, out_ref, send_sem, recv_sem):
    me = greet(axis, count)
    copies = []
    for step in range(1, count):
        copies.append(
            pltpu.make_async_remote_copy(
                src_ref=x_ref,
                dst_ref=out_ref.at[me],
                send_sem=send_sem.at[step - 1],
                recv_sem=recv_sem.at[step - 1],
                device_id={axis: lax.rem(me + step, count)},
                device_id_type=MESH,
            )
        )
        copies[-1].start()
    out_ref[me] = x_ref[...]
    for copy in copies:
        copy.wait()


def all_gather(x, axis, collective_id):
    count = lax.axis_size(axis)
    return pl.pallas_call(
        functools.partial(all_gather_kernel, axis, count),
        out_shape=jax.ShapeDtypeStruct((count,) + x.shape, x.dtype),
        in_specs=[pl.BlockSpec(memory_space=pltpu.VMEM)],
        out_specs=pl.BlockSpec(memory_space=pltpu.VMEM),
        scratch_shapes=[pltpu.SemaphoreType.DMA((count - 1,))] * 2,
        compiler_params=pltpu.CompilerParams(
            collective_id=collective_id, has_side_effects=True, vmem_limit_bytes=BIG
        ),
    )(x)


def flatten_kernel(tiles, x_ref, out_ref):
    rows, size = out_ref.shape[0], x_ref.shape[1]
    for tile in range(tiles):
        out_ref[:, tile * size : (tile + 1) * size] = x_ref[pl.ds(tile, rows, stride=tiles), :]


def flatten(matrix_tiles):
    block_rows, _, tile_size, block_cols, _, width = matrix_tiles.shape
    flat = matrix_tiles.reshape(block_rows * tile_size * block_cols, width)
    return pl.pallas_call(
        functools.partial(flatten_kernel, block_cols),
        grid=(block_rows,),
        in_specs=[pl.BlockSpec((tile_size * block_cols, width), lambda i: (i, 0))],
        out_specs=pl.BlockSpec((tile_size, block_cols * width), lambda i: (i, 0)),
        out_shape=jax.ShapeDtypeStruct(
            (block_rows * tile_size, block_cols * width), matrix_tiles.dtype
        ),
        compiler_params=pltpu.CompilerParams(vmem_limit_bytes=BIG),
    )(flat)


def split(value):
    high = value.astype(jnp.bfloat16)
    return high, (value - high.astype(jnp.float32)).astype(jnp.bfloat16)


def update_kernel(tiles, flat, x_ref, left_ref, right_ref, out_ref, high_ref, low_ref):
    rows = x_ref.shape[0]
    size = x_ref.shape[1] // tiles

    @pl.when(pl.program_id(0) == 0)
    def _():
        high_ref[...], low_ref[...] = split(right_ref[...])

    left_high, left_low = split(left_ref[...])
    group = 2 if tiles % 2 == 0 else 1
    for first in range(0, tiles, group):
        part = slice(first * size, (first + group) * size)
        right_high, right_low = high_ref[part, :], low_ref[part, :]
        dot = lambda a, b: lax.dot_general(
            a, b, (((1,), (1,)), ((), ())), preferred_element_type=jnp.float32
        )
        product = dot(left_high, right_high) + (
            dot(left_high, right_low) + dot(left_low, right_high)
        )
        value = x_ref[:, part] - product
        if not flat:
            out_ref[:, part] = value
            continue
        for offset in range(group):
            out_ref[pl.ds(first + offset, rows, stride=tiles), :] = value[
                :, offset * size : (offset + 1) * size
            ]


def update(matrix, left, right, tiles, flat):
    row_count, col_count = matrix.shape
    size = col_count // tiles
    blocks = row_count // size
    rows = size * (2 if blocks % 2 == 0 else 1)
    depth = left.shape[1]
    wide = pl.BlockSpec((rows, col_count), lambda i: (i, 0))
    return pl.pallas_call(
        functools.partial(update_kernel, tiles, flat),
        grid=(row_count // rows,),
        in_specs=[
            wide,
            pl.BlockSpec((rows, depth), lambda i: (i, 0)),
            pl.BlockSpec((col_count, depth), lambda i: (0, 0), pipeline_mode=pl.Buffered(1)),
        ],
        out_specs=pl.BlockSpec((rows * tiles, size), lambda i: (i, 0)) if flat else wide,
        out_shape=jax.ShapeDtypeStruct(
            (row_count * tiles, size) if flat else matrix.shape, matrix.dtype
        ),
        scratch_shapes=[pltpu.VMEM((col_count, depth), jnp.bfloat16)] * 2,
        compiler_params=pltpu.CompilerParams(vmem_limit_bytes=BIG),
    )(matrix, left, right)


def mirror_order(pieces, block_rows, tile_size):
    stacked = jnp.stack(pieces, 0)
    stacked = stacked.reshape(len(pieces), block_rows, tile_size, stacked.shape[-1])
    return stacked.transpose(1, 0, 2, 3).reshape(-1, stacked.shape[-1])


def on_device(matrix_tiles):
    tile_shape = matrix_tiles.shape
    block_rows, _, tile_size, block_cols = tile_shape[:4]
    row_count = block_rows * tile_size
    col_count = block_cols * tile_size
    row_devices = lax.axis_size("row")
    col_devices = lax.axis_size("col")
    row_ratio = row_devices // col_devices
    row_index = lax.axis_index("row")
    col_index = lax.axis_index("col")

    def positions(count, devices, index):
        place = jnp.arange(count, dtype=jnp.int32)
        return (place // tile_size * devices + index) * tile_size + place % tile_size

    global_rows = positions(row_count, row_devices, row_index)
    global_cols = positions(col_count, col_devices, col_index)
    band_columns = jnp.arange(BAND, dtype=jnp.int32)
    panel_tiles = BAND // tile_size
    high = lax.Precision.HIGH

    def row_tiles(source, first):
        blocks = []
        for tile in range(first, first + panel_tiles):
            local_tile = tile // row_devices
            part = source[local_tile * tile_size : (local_tile + 1) * tile_size]
            blocks.append(jnp.where(row_index == tile % row_devices, part, 0.0))
        return jnp.concatenate(blocks, 0)

    matrix = flatten(matrix_tiles)
    held = -(-PANELS * panel_tiles // col_devices)
    gathered = all_gather(matrix[:, : held * tile_size], "col", 0)
    panels_rows, panels_cols = [], []
    for panel_index in range(PANELS):
        pieces = []
        for tile in range(panel_index * panel_tiles, (panel_index + 1) * panel_tiles):
            local_tile = tile // col_devices
            pieces.append(
                gathered[
                    tile % col_devices, :, local_tile * tile_size : (local_tile + 1) * tile_size
                ]
            )
        panels_rows.append(jnp.concatenate(pieces, 1))
        sent = row_tiles(matrix, panel_index * panel_tiles)
        if panels_cols:
            sent, panels_cols[-1] = lax.optimization_barrier((sent, panels_cols[-1]))
        panels_cols.append(lax.psum(sent, "row"))

    lefts, rights = [], []
    for panel_index in range(PANELS):
        below_start = (panel_index + 1) * BAND
        last = panel_index == PANELS - 1
        panel_rows = jnp.where((global_rows >= below_start)[:, None], panels_rows[panel_index], 0.0)
        stacked = jnp.concatenate(
            [
                multiply(panel_rows, panel_rows, 0, 0),
                row_tiles(panel_rows, below_start // tile_size),
            ],
            0,
        )
        stacked = share(stacked, 1)
        inverse, shifted, transform, signs = factors(stacked[:BAND], stacked[BAND:])

        def reflectors(panel, places):
            on_sign = (places[:, None] - below_start == band_columns[None, :]).astype(jnp.float32)
            return multiply(panel, inverse, 1, 1) - on_sign * signs

        vec_rows = reflectors(panel_rows, global_rows)
        panel_cols = jnp.where((global_cols >= below_start)[:, None], panels_cols[panel_index].T, 0.0)
        vec_cols = reflectors(panel_cols, global_cols)
        partial = multiply(matrix, vec_cols, precision=high)
        if lefts:
            left, right = jnp.concatenate(lefts, 1), jnp.concatenate(rights, 1)
            partial = partial - multiply(
                left, multiply(right, vec_cols, 0, 0, precision=high), precision=high
            )
        applied = multiply(all_reduce(partial, "col", 2), transform)
        moved = applied
        if not last:
            moved, panels_cols[panel_index + 1] = lax.optimization_barrier(
                (applied, panels_cols[panel_index + 1])
            )
        pieces = []
        for part_index in range(row_ratio):
            mine = row_index == col_index + col_devices * part_index
            pieces.append(lax.psum(jnp.where(mine, moved, 0.0), "row"))
        applied_cols = mirror_order(pieces, block_rows, tile_size)
        inner_part = multiply(vec_rows, applied, 0, 0)
        if last:
            inner = share(inner_part, 3)
        else:
            stacked = jnp.concatenate([inner_part, row_tiles(applied, below_start // tile_size)], 0)
            stacked = share(stacked, 1)
            inner = stacked[:BAND]
        half_inner = 0.5 * multiply(transform, inner, 0, 0)
        update_rows = applied - multiply(vec_rows, half_inner)
        update_cols = applied_cols - multiply(vec_cols, half_inner)
        lefts += [vec_rows, update_rows]
        rights += [update_cols, vec_cols]
        if not last:
            update_next = stacked[BAND:] - multiply(shifted, half_inner)
            panels_rows[panel_index + 1] = (
                panels_rows[panel_index + 1]
                - multiply(vec_rows, update_next, 1, 1)
                - multiply(update_rows, shifted, 1, 1)
            )
            panels_cols[panel_index + 1] = (
                panels_cols[panel_index + 1]
                - multiply(update_next, vec_cols, 1, 1)
                - multiply(shifted, update_cols, 1, 1)
            )
    early = len(lefts) - 2
    order = [index for index in range(len(lefts)) if index != early]
    matrix = update(
        matrix,
        jnp.concatenate([lefts[index] for index in order], 1),
        jnp.concatenate([rights[index] for index in order], 1),
        block_cols,
        False,
    )
    return update(matrix, lefts[early], rights[early], block_cols, True).reshape(tile_shape)


def solution(mesh):
    return jax.shard_map(
        on_device,
        mesh=mesh,
        in_specs=(P(None, "row", None, None, "col", None),),
        out_specs=P(None, "row", None, None, "col", None),
        check_vma=False,
    )
```

```python
import functools

import jax
import jax.numpy as jnp
from jax import lax
from jax.experimental import pallas as pl
from jax.experimental.pallas import tpu as pltpu
from jax.sharding import PartitionSpec as P

BAND = 256
PANELS = 2
BIG = 60 * 1024 * 1024
MESH = pl.DeviceIdType.MESH

HI = lax.Precision.HIGHEST
def mm(a, b, ca, cb):
    return lax.dot_general(a, b, (((ca,), (cb,)), ((), ())), precision=HI, preferred_element_type=jnp.float32)

def base_inverse(block):
    size = block.shape[0]
    wide = (8, 2 * size)
    group = 8
    places = lax.broadcasted_iota(jnp.int32, wide, 0)
    cols = lax.broadcasted_iota(jnp.int32, wide, 1)
    work = []
    for k in range(size // 8):
        unit = jnp.where(places + 8 * k == cols, 1.0, 0.0)[:, :size]
        work.append(jnp.concatenate([block[8 * k : 8 * k + 8], unit], 1))
    for start in range(0, size, group):
        own, offset = divmod(start, 8)
        rows = [jnp.broadcast_to(work[own][offset + i : offset + i + 1], wide) for i in range(group)]
        pivot = [
            [jnp.broadcast_to(rows[i][:, start + j : start + j + 1], wide) for j in range(group)]
            for i in range(group)
        ]
        first = own if offset + group < 8 else own + 1
        columns = [
            [jnp.broadcast_to(work[k][:, start + i : start + i + 1], wide) for i in range(group)]
            for k in range(first, len(work))
        ]
        scaled = []
        for i in range(group):
            inverse = 1.0 / pivot[i][i]
            scaled.append(rows[i] * inverse)
            for j in range(i + 1, group):
                ratio = pivot[i][j] * inverse
                for l in range(j, group):
                    pivot[j][l] = pivot[j][l] - ratio * pivot[i][l]
                rows[j] = rows[j] - ratio * rows[i]
                for column in columns:
                    column[j] = column[j] - ratio * column[i]
        for k, column in zip(range(first, len(work)), columns):
            change = column[0] * scaled[0]
            for i in range(1, group):
                change = change + column[i] * scaled[i]
            if k == own:
                change = jnp.where(places >= offset + group, change, 0.0)
            work[k] = work[k] - change
        for i in range(group):
            work[own] = jnp.where(places == offset + i, rows[i], work[own])
    result = []
    for k, value in enumerate(work):
        pivots = jnp.sum(jnp.where(places + 8 * k == cols, value, 0.0), axis=1, keepdims=True)
        result.append(value[:, size:] * (1.0 / jnp.sqrt(pivots)))
    return jnp.concatenate(result, 0)


def factor_inverse(matrix, base):
    size = matrix.shape[0]
    if size <= base:
        return base_inverse(matrix)
    half = size // 2
    first = factor_inverse(matrix[:half, :half], base)
    lower = mm(matrix[half:, :half], first, 1, 1)
    second = factor_inverse(matrix[half:, half:] - mm(lower, lower, 1, 1), base)
    corner = -mm(second, mm(lower, first, 1, 0), 1, 0)
    top = jnp.concatenate([first, jnp.zeros_like(first)], 1)
    return jnp.concatenate([top, jnp.concatenate([corner, second], 1)], 0)

def factor_kernel(gram_ref, top_ref, inverse_ref, shifted_ref, transform_ref, sign_ref):
    size = gram_ref.shape[0]
    inverse = factor_inverse(gram_ref[...], 64)
    inverse_ref[...] = inverse
    basis = mm(top_ref[...], inverse, 1, 1)
    rows = lax.broadcasted_iota(jnp.int32, (size, size), 0)
    cols = lax.broadcasted_iota(jnp.int32, (size, size), 1)
    on_diagonal = rows == cols
    sign_square = jnp.where(on_diagonal, jnp.where(basis >= 0, -1.0, 1.0), 0.0)
    shifted = basis - sign_square
    shifted_ref[...] = shifted
    outer = factor_inverse(mm(shifted, shifted, 0, 0), 64)
    sign_column = jnp.sum(sign_square, axis=1, keepdims=True)
    transform_ref[...] = -sign_column * mm(mm(shifted, outer, 1, 1), outer, 1, 0)
    sign_ref[...] = jnp.sum(sign_square, axis=0, keepdims=True)


def factors(gram, top):
    size = gram.shape[0]
    square = jax.ShapeDtypeStruct((size, size), jnp.float32)
    return pl.pallas_call(
        factor_kernel,
        out_shape=(square, square, square, jax.ShapeDtypeStruct((1, size), jnp.float32)),
    )(gram, top)


def multiply(first, second, first_dim=1, second_dim=0, precision=HI):
    return lax.dot_general(
        first,
        second,
        (((first_dim,), (second_dim,)), ((), ())),
        precision=precision,
        preferred_element_type=jnp.float32,
    )


def greet(axis, count):
    me = lax.axis_index(axis)
    barrier = pltpu.get_barrier_semaphore()
    for step in range(1, count):
        pl.semaphore_signal(
            barrier, inc=1, device_id={axis: lax.rem(me + step, count)}, device_id_type=MESH
        )
    pl.semaphore_wait(barrier, count - 1)
    return me


def all_reduce_kernel(axis, count, x_ref, out_ref, parts, send_sem, recv_sem, send_two, recv_two):
    me = greet(axis, count)
    copies = []
    for step in range(1, count):
        peer = lax.rem(me + step, count)
        copies.append(
            pltpu.make_async_remote_copy(
                src_ref=x_ref.at[peer],
                dst_ref=parts.at[step - 1],
                send_sem=send_sem.at[step - 1],
                recv_sem=recv_sem.at[step - 1],
                device_id={axis: peer},
                device_id_type=MESH,
            )
        )
        copies[-1].start()
    total = x_ref[me]
    for step in range(1, count):
        copies[step - 1].wait_recv()
        total = total + parts[step - 1]
    out_ref[me] = total
    second = []
    for step in range(1, count):
        peer = lax.rem(me + step, count)
        second.append(
            pltpu.make_async_remote_copy(
                src_ref=out_ref.at[me],
                dst_ref=out_ref.at[me],
                send_sem=send_two.at[step - 1],
                recv_sem=recv_two.at[step - 1],
                device_id={axis: peer},
                device_id_type=MESH,
            )
        )
        second[-1].start()
    for copy in copies:
        copy.wait_send()
    for copy in second:
        copy.wait()


def all_reduce(x, axis, collective_id):
    count = lax.axis_size(axis)
    rows, cols = x.shape
    pieces = (count, rows // count, cols)
    out = pl.pallas_call(
        functools.partial(all_reduce_kernel, axis, count),
        out_shape=jax.ShapeDtypeStruct(pieces, x.dtype),
        in_specs=[pl.BlockSpec(memory_space=pltpu.VMEM)],
        out_specs=pl.BlockSpec(memory_space=pltpu.VMEM),
        scratch_shapes=[pltpu.VMEM((count - 1,) + pieces[1:], x.dtype)]
        + [pltpu.SemaphoreType.DMA((count - 1,))] * 4,
        compiler_params=pltpu.CompilerParams(
            collective_id=collective_id, has_side_effects=True, vmem_limit_bytes=BIG
        ),
    )(x.reshape(pieces))
    return out.reshape(rows, cols)


def share_kernel(rows, cols, x_ref, out_ref, parts, send_sem, recv_sem, send_two, recv_two, send_col, recv_col):
    row_me = lax.axis_index("row")
    col_me = lax.axis_index("col")
    barrier = pltpu.get_barrier_semaphore()
    for axis, me, count in (("row", row_me, rows), ("col", col_me, cols)):
        for step in range(1, count):
            pl.semaphore_signal(
                barrier, inc=1, device_id={axis: lax.rem(me + step, count)}, device_id_type=MESH
            )
    pl.semaphore_wait(barrier, rows + cols - 2)

    def send(source, target, axis, peer, out_sem, in_sem):
        copy = pltpu.make_async_remote_copy(
            src_ref=source,
            dst_ref=target,
            send_sem=out_sem,
            recv_sem=in_sem,
            device_id={axis: peer},
            device_id_type=MESH,
        )
        copy.start()
        return copy

    first, second, third = [], [], []
    for step in range(1, rows):
        peer = lax.rem(row_me + step, rows)
        slot = step - 1
        first.append(
            send(x_ref.at[col_me, peer], parts.at[slot], "row", peer, send_sem.at[slot], recv_sem.at[slot])
        )
    total = x_ref[col_me, row_me]
    for step in range(1, rows):
        first[step - 1].wait_recv()
        total = total + parts[step - 1]
    out_ref[col_me, row_me] = total
    mine = out_ref.at[col_me, row_me]
    for step in range(1, rows):
        peer = lax.rem(row_me + step, rows)
        slot = step - 1
        second.append(send(mine, mine, "row", peer, send_two.at[slot], recv_two.at[slot]))
    for copy in second:
        copy.wait_recv()
    mine = out_ref.at[col_me]
    for step in range(1, cols):
        peer = lax.rem(col_me + step, cols)
        slot = step - 1
        third.append(send(mine, mine, "col", peer, send_col.at[slot], recv_col.at[slot]))
    for copy in first + second:
        copy.wait_send()
    for copy in third:
        copy.wait()


def share(x, collective_id):
    rows, cols = lax.axis_size("row"), lax.axis_size("col")
    size, width = x.shape
    pieces = (cols, rows, size // (rows * cols), width)
    out = pl.pallas_call(
        functools.partial(share_kernel, rows, cols),
        out_shape=jax.ShapeDtypeStruct(pieces, x.dtype),
        in_specs=[pl.BlockSpec(memory_space=pltpu.VMEM)],
        out_specs=pl.BlockSpec(memory_space=pltpu.VMEM),
        scratch_shapes=[pltpu.VMEM((rows - 1,) + pieces[2:], x.dtype)]
        + [pltpu.SemaphoreType.DMA((rows - 1,))] * 4
        + [pltpu.SemaphoreType.DMA((cols - 1,))] * 2,
        compiler_params=pltpu.CompilerParams(
            collective_id=collective_id, has_side_effects=True, vmem_limit_bytes=BIG
        ),
    )(x.reshape(pieces))
    return out.reshape(size, width)


def all_gather_kernel(axis, count, x_ref, out_ref, send_sem, recv_sem):
    me = greet(axis, count)
    copies = []
    for step in range(1, count):
        copies.append(
            pltpu.make_async_remote_copy(
                src_ref=x_ref,
                dst_ref=out_ref.at[me],
                send_sem=send_sem.at[step - 1],
                recv_sem=recv_sem.at[step - 1],
                device_id={axis: lax.rem(me + step, count)},
                device_id_type=MESH,
            )
        )
        copies[-1].start()
    out_ref[me] = x_ref[...]
    for copy in copies:
        copy.wait()


def all_gather(x, axis, collective_id):
    count = lax.axis_size(axis)
    return pl.pallas_call(
        functools.partial(all_gather_kernel, axis, count),
        out_shape=jax.ShapeDtypeStruct((count,) + x.shape, x.dtype),
        in_specs=[pl.BlockSpec(memory_space=pltpu.VMEM)],
        out_specs=pl.BlockSpec(memory_space=pltpu.VMEM),
        scratch_shapes=[pltpu.SemaphoreType.DMA((count - 1,))] * 2,
        compiler_params=pltpu.CompilerParams(
            collective_id=collective_id, has_side_effects=True, vmem_limit_bytes=BIG
        ),
    )(x)


def flatten_kernel(tiles, x_ref, out_ref):
    rows, size = out_ref.shape[0], x_ref.shape[1]
    for tile in range(tiles):
        out_ref[:, tile * size : (tile + 1) * size] = x_ref[pl.ds(tile, rows, stride=tiles), :]


def flatten(matrix_tiles):
    block_rows, _, tile_size, block_cols, _, width = matrix_tiles.shape
    flat = matrix_tiles.reshape(block_rows * tile_size * block_cols, width)
    return pl.pallas_call(
        functools.partial(flatten_kernel, block_cols),
        grid=(block_rows,),
        in_specs=[pl.BlockSpec((tile_size * block_cols, width), lambda i: (i, 0))],
        out_specs=pl.BlockSpec((tile_size, block_cols * width), lambda i: (i, 0)),
        out_shape=jax.ShapeDtypeStruct(
            (block_rows * tile_size, block_cols * width), matrix_tiles.dtype
        ),
        compiler_params=pltpu.CompilerParams(vmem_limit_bytes=BIG),
    )(flat)


def split(value):
    high = value.astype(jnp.bfloat16)
    return high, (value - high.astype(jnp.float32)).astype(jnp.bfloat16)


def update_kernel(tiles, flat, x_ref, left_ref, right_ref, out_ref, high_ref, low_ref):
    rows = x_ref.shape[0]
    size = x_ref.shape[1] // tiles

    @pl.when(pl.program_id(0) == 0)
    def _():
        high_ref[...], low_ref[...] = split(right_ref[...])

    left_high, left_low = split(left_ref[...])
    group = 2 if tiles % 2 == 0 else 1
    for first in range(0, tiles, group):
        part = slice(first * size, (first + group) * size)
        right_high, right_low = high_ref[part, :], low_ref[part, :]
        dot = lambda a, b: lax.dot_general(
            a, b, (((1,), (1,)), ((), ())), preferred_element_type=jnp.float32
        )
        product = dot(left_high, right_high) + (
            dot(left_high, right_low) + dot(left_low, right_high)
        )
        value = x_ref[:, part] - product
        if not flat:
            out_ref[:, part] = value
            continue
        for offset in range(group):
            out_ref[pl.ds(first + offset, rows, stride=tiles), :] = value[
                :, offset * size : (offset + 1) * size
            ]


def update(matrix, left, right, tiles, flat):
    row_count, col_count = matrix.shape
    size = col_count // tiles
    blocks = row_count // size
    rows = size * (2 if blocks % 2 == 0 else 1)
    depth = left.shape[1]
    wide = pl.BlockSpec((rows, col_count), lambda i: (i, 0))
    return pl.pallas_call(
        functools.partial(update_kernel, tiles, flat),
        grid=(row_count // rows,),
        in_specs=[
            wide,
            pl.BlockSpec((rows, depth), lambda i: (i, 0)),
            pl.BlockSpec((col_count, depth), lambda i: (0, 0), pipeline_mode=pl.Buffered(1)),
        ],
        out_specs=pl.BlockSpec((rows * tiles, size), lambda i: (i, 0)) if flat else wide,
        out_shape=jax.ShapeDtypeStruct(
            (row_count * tiles, size) if flat else matrix.shape, matrix.dtype
        ),
        scratch_shapes=[pltpu.VMEM((col_count, depth), jnp.bfloat16)] * 2,
        compiler_params=pltpu.CompilerParams(vmem_limit_bytes=BIG),
    )(matrix, left, right)


def mirror_order(pieces, block_rows, tile_size):
    stacked = jnp.stack(pieces, 0)
    stacked = stacked.reshape(len(pieces), block_rows, tile_size, stacked.shape[-1])
    return stacked.transpose(1, 0, 2, 3).reshape(-1, stacked.shape[-1])


def on_device(matrix_tiles):
    tile_shape = matrix_tiles.shape
    block_rows, _, tile_size, block_cols = tile_shape[:4]
    row_count = block_rows * tile_size
    col_count = block_cols * tile_size
    row_devices = lax.axis_size("row")
    col_devices = lax.axis_size("col")
    row_ratio = row_devices // col_devices
    row_index = lax.axis_index("row")
    col_index = lax.axis_index("col")

    def positions(count, devices, index):
        place = jnp.arange(count, dtype=jnp.int32)
        return (place // tile_size * devices + index) * tile_size + place % tile_size

    global_rows = positions(row_count, row_devices, row_index)
    global_cols = positions(col_count, col_devices, col_index)
    band_columns = jnp.arange(BAND, dtype=jnp.int32)
    panel_tiles = BAND // tile_size
    high = lax.Precision.HIGH

    def row_tiles(source, first):
        blocks = []
        for tile in range(first, first + panel_tiles):
            local_tile = tile // row_devices
            part = source[local_tile * tile_size : (local_tile + 1) * tile_size]
            blocks.append(jnp.where(row_index == tile % row_devices, part, 0.0))
        return jnp.concatenate(blocks, 0)

    matrix = flatten(matrix_tiles)
    held = -(-PANELS * panel_tiles // col_devices)
    gathered = all_gather(matrix[:, : held * tile_size], "col", 0)
    panels_rows, panels_cols = [], []
    for panel_index in range(PANELS):
        pieces = []
        for tile in range(panel_index * panel_tiles, (panel_index + 1) * panel_tiles):
            local_tile = tile // col_devices
            pieces.append(
                gathered[
                    tile % col_devices, :, local_tile * tile_size : (local_tile + 1) * tile_size
                ]
            )
        panels_rows.append(jnp.concatenate(pieces, 1))
        sent = row_tiles(matrix, panel_index * panel_tiles)
        if panels_cols:
            sent, panels_cols[-1] = lax.optimization_barrier((sent, panels_cols[-1]))
        panels_cols.append(lax.psum(sent, "row"))

    lefts, rights = [], []
    for panel_index in range(PANELS):
        below_start = (panel_index + 1) * BAND
        last = panel_index == PANELS - 1
        panel_rows = jnp.where((global_rows >= below_start)[:, None], panels_rows[panel_index], 0.0)
        stacked = jnp.concatenate(
            [
                multiply(panel_rows, panel_rows, 0, 0),
                row_tiles(panel_rows, below_start // tile_size),
            ],
            0,
        )
        stacked = share(stacked, 1)
        inverse, shifted, transform, signs = factors(stacked[:BAND], stacked[BAND:])

        def reflectors(panel, places):
            on_sign = (places[:, None] - below_start == band_columns[None, :]).astype(jnp.float32)
            return multiply(panel, inverse, 1, 1) - on_sign * signs

        vec_rows = reflectors(panel_rows, global_rows)
        panel_cols = jnp.where((global_cols >= below_start)[:, None], panels_cols[panel_index].T, 0.0)
        vec_cols = reflectors(panel_cols, global_cols)
        partial = multiply(matrix, vec_cols, precision=high)
        if lefts:
            left, right = jnp.concatenate(lefts, 1), jnp.concatenate(rights, 1)
            partial = partial - multiply(
                left, multiply(right, vec_cols, 0, 0, precision=high), precision=high
            )
        applied = multiply(all_reduce(partial, "col", 2), transform)
        moved = applied
        if not last:
            moved, panels_cols[panel_index + 1] = lax.optimization_barrier(
                (applied, panels_cols[panel_index + 1])
            )
        pieces = []
        for part_index in range(row_ratio):
            mine = row_index == col_index + col_devices * part_index
            pieces.append(lax.psum(jnp.where(mine, moved, 0.0), "row"))
        applied_cols = mirror_order(pieces, block_rows, tile_size)
        inner_part = multiply(vec_rows, applied, 0, 0)
        if last:
            inner = share(inner_part, 3)
        else:
            stacked = jnp.concatenate([inner_part, row_tiles(applied, below_start // tile_size)], 0)
            stacked = share(stacked, 1)
            inner = stacked[:BAND]
        half_inner = 0.5 * multiply(transform, inner, 0, 0)
        update_rows = applied - multiply(vec_rows, half_inner)
        update_cols = applied_cols - multiply(vec_cols, half_inner)
        lefts += [vec_rows, update_rows]
        rights += [update_cols, vec_cols]
        if not last:
            update_next = stacked[BAND:] - multiply(shifted, half_inner)
            panels_rows[panel_index + 1] = (
                panels_rows[panel_index + 1]
                - multiply(vec_rows, update_next, 1, 1)
                - multiply(update_rows, shifted, 1, 1)
            )
            panels_cols[panel_index + 1] = (
                panels_cols[panel_index + 1]
                - multiply(update_next, vec_cols, 1, 1)
                - multiply(shifted, update_cols, 1, 1)
            )
    early = len(lefts) - 2
    order = [index for index in range(len(lefts)) if index != early]
    matrix = update(
        matrix,
        jnp.concatenate([lefts[index] for index in order], 1),
        jnp.concatenate([rights[index] for index in order], 1),
        block_cols,
        False,
    )
    return update(matrix, lefts[early], rights[early], block_cols, True).reshape(tile_shape)


def solution(mesh):
    return jax.shard_map(
        on_device,
        mesh=mesh,
        in_specs=(P(None, "row", None, None, "col", None),),
        out_specs=P(None, "row", None, None, "col", None),
        check_vma=False,
    )
```
